128 devices in a mesh: seq: 16 (over z, x), head: 8 (over y, core).
Axes of the slice: x: 4, y: 4, z: 4, core: 2. Of those that a mesh axis runs over, the one named last changes fastest.
Arguments:
- queries: bfloat16 [8192, 4096], P('seq', 'head'), may hold values from -12 to 12
- keys: bfloat16 [8192, 4096], P('seq', 'head'), may hold values from -6 to 6
- values: bfloat16 [8192, 4096], P('seq', 'head'), may hold values from -6 to 6
- out_grad: bfloat16 [8192, 4096], P('seq', 'head'), may hold values from -6 to 6
- out_weight: bfloat16 [4096, 4096], P('head'), may hold values from -0.09375 to 0.09375
- rand_blocks: int32 [32, 128, 3], P('head'), may hold values from 0 to 127, as said below
- glob_blocks: int32 [2], replicated, may hold values from 0 to 127, as said below
Outputs:
- query_grad: bfloat16 [8192, 4096], P('seq', 'head')
- key_grad: bfloat16 [8192, 4096], P('seq', 'head')
- value_grad: bfloat16 [8192, 4096], P('seq', 'head')
The draws below stay inside these ranges and needn't reach their ends.
Inputs may be any that keep to these rules, and one draw needn't show every extreme that they name: `glob_blocks`: distinct block numbers; the last entry is always the sequence's last block, 127. `rand_blocks`: count the random blocks that the query blocks of one index of seq name for the heads of one index of head: at most 9 of these 96 lie among the blocks held by any one index of seq; and for each index of head there is one index of seq (the same for all requesters) whose blocks receive exactly 9 of the 96 requests from every index of seq.
All inputs are finite; a program needn't handle non-finite values.
Results may differ from the reference program's by a relative error of at most 0.0075.
Values may be sent and summed in bfloat16 or wider, within the bound.
No kernel may reach another device: no remote copies, remote signals or barrier semaphores. Data moves between devices by JAX's collectives and lax.ppermute only.
A program may use at most 256 MiB of HBM per device.

```python
import math
import jax
import jax.numpy as jnp
from jax import lax

HEADS = 32
HEAD_FEATURES = 128
BLOCK_TOKENS = 64
RANDOMS = 3
GLOBALS = 2
D = 4096
TOKENS = 8192
HEADS_DEV = 4
BLOCKS_DEV = 8
SEQUENCE_BLOCKS = 128
REQUESTS = 96
CAPACITY = 9
N_SEQ = 16


def owner_pattern(pattern_key, hot_owner):
    subkeys = jax.random.split(pattern_key, 3)
    ordering = jax.random.permutation(subkeys[0], REQUESTS)
    others = (hot_owner + 1 + jax.random.permutation(subkeys[1], N_SEQ - 1)) % N_SEQ
    rest_index = jnp.arange(REQUESTS - CAPACITY) % (N_SEQ - 1)
    owners = jnp.zeros((REQUESTS,), jnp.int32)
    owners = owners.at[ordering[:CAPACITY]].set(hot_owner.astype(jnp.int32))
    owners = owners.at[ordering[CAPACITY:]].set(others[rest_index].astype(jnp.int32))
    within = jax.random.randint(subkeys[2], (REQUESTS,), 0, BLOCKS_DEV)
    return (owners * BLOCKS_DEV + within).astype(jnp.int32)


def group_pattern(group_key):
    hot_owner = jax.random.randint(jax.random.fold_in(group_key, 1), (), 0, N_SEQ)
    device_keys = jax.random.split(jax.random.fold_in(group_key, 2), N_SEQ)

    def one_device(device_key):
        return owner_pattern(device_key, hot_owner)
    return jax.vmap(one_device)(device_keys)


def draw_rand_blocks(key, part):
    groups = HEADS // HEADS_DEV
    group_keys = jax.random.split(jax.random.fold_in(key, 11), groups)
    blocks_table = jax.vmap(group_pattern)(group_keys)
    blocks_table = blocks_table.reshape(groups, N_SEQ, HEADS_DEV, BLOCKS_DEV, RANDOMS)
    return blocks_table.transpose(0, 2, 1, 3, 4).reshape(HEADS, SEQUENCE_BLOCKS, RANDOMS).astype(jnp.int32)


def draw_glob_blocks(key, part):
    earlier = jax.random.permutation(jax.random.fold_in(key, 5), SEQUENCE_BLOCKS - 1)[:GLOBALS - 1].astype(jnp.int32)
    last_block = jnp.full((1,), SEQUENCE_BLOCKS - 1, jnp.int32)
    return jnp.concatenate([earlier, last_block]).astype(jnp.int32)


def block_scale(own_key, dims, shards, low, largest):
    loudness, own = 1.0, jax.random.fold_in(own_key, 6)
    for axis_at, blocks in shards:
        heights = jnp.exp(jax.random.uniform(jax.random.fold_in(own, axis_at), (blocks,), jnp.float32, low / len(shards), largest / len(shards)))
        loudness = loudness * jnp.repeat(heights, dims[axis_at] // blocks).reshape([-1 if axis == axis_at else 1 for axis in range(len(dims))])
    return loudness


def bell_draw(rng, shape, spread, most, shards=(), kind=jnp.bfloat16):
    loudness = block_scale(rng, shape, shards, -0.22, 0.18) if shards else 1.0
    drawn = jax.random.normal(rng, shape, jnp.float32) * spread * loudness
    return jnp.minimum(jnp.maximum(drawn, -most), most).astype(kind)


def setup_inputs(seed: int = 0) -> dict:
    streams_of = jax.random.split(jax.random.key(seed), 8)
    queries = bell_draw(streams_of[0], (TOKENS, D), 2.0, 12.0, ((0, 16), (1, 8)))
    keys = bell_draw(streams_of[1], (TOKENS, D), 1.0, 6.0, ((0, 16), (1, 8)))
    values = bell_draw(streams_of[2], (TOKENS, D), 1.0, 6.0, ((0, 16), (1, 8)))
    out_grad = bell_draw(streams_of[3], (TOKENS, D), 1.0, 6.0, ((0, 16), (1, 8)))
    out_weight = bell_draw(streams_of[4], (D, D), D ** -0.5, 0.09375, ((0, 8),))
    rand_blocks = draw_rand_blocks(jax.random.fold_in(streams_of[7], 71), 0)
    glob_blocks = draw_glob_blocks(jax.random.fold_in(streams_of[7], 71), 0)
    return {"queries": queries, "keys": keys, "values": values, "out_grad": out_grad, "out_weight": out_weight, "rand_blocks": rand_blocks, "glob_blocks": glob_blocks}


def attend_head(query_rows, key_rows, value_rows, grad_rows, random_row, glob_blocks, is_global):
    scale_factor = 1.0 / math.sqrt(HEAD_FEATURES)
    listed_total_count = 3 + GLOBALS + RANDOMS
    query_blocks = query_rows.reshape(SEQUENCE_BLOCKS, BLOCK_TOKENS, HEAD_FEATURES)
    grad_blocks = grad_rows.reshape(SEQUENCE_BLOCKS, BLOCK_TOKENS, HEAD_FEATURES)
    key_padded = jnp.pad(key_rows.reshape(SEQUENCE_BLOCKS, BLOCK_TOKENS, HEAD_FEATURES), ((1, 1), (0, 0), (0, 0)))
    value_padded = jnp.pad(value_rows.reshape(SEQUENCE_BLOCKS, BLOCK_TOKENS, HEAD_FEATURES), ((1, 1), (0, 0), (0, 0)))
    position = jnp.arange(SEQUENCE_BLOCKS, dtype=jnp.int32)
    offsets = jnp.arange(3, dtype=jnp.int32)
    window = position[:, None] + offsets[None, :]
    inside = (window >= 1) & (window <= SEQUENCE_BLOCKS)
    glob_cols = jnp.broadcast_to(glob_blocks[None, :] + 1, (SEQUENCE_BLOCKS, GLOBALS))
    listed = jnp.concatenate([window, glob_cols, random_row + 1], axis=1).astype(jnp.int32)
    live = jnp.concatenate([inside, jnp.ones((SEQUENCE_BLOCKS, GLOBALS + RANDOMS), dtype=bool)], axis=1)
    live_cols = jnp.repeat(live, BLOCK_TOKENS, axis=1).astype(jnp.float32)
    listed_keys = key_padded[listed].reshape(SEQUENCE_BLOCKS, listed_total_count * BLOCK_TOKENS, HEAD_FEATURES).astype(jnp.float32)
    listed_values = value_padded[listed].reshape(SEQUENCE_BLOCKS, listed_total_count * BLOCK_TOKENS, HEAD_FEATURES).astype(jnp.float32)
    query_single = query_blocks.astype(jnp.float32)
    masked_grad = jnp.where(is_global[:, None, None], jnp.zeros_like(grad_blocks), grad_blocks)
    gradient_single = masked_grad.astype(jnp.float32)
    attention_scores = jnp.einsum('vwi,vri->vwr', query_single, listed_keys) * scale_factor
    weights_raw = jnp.exp(attention_scores) * live_cols[:, None, :]
    probs = weights_raw / lax.optimization_barrier(jnp.sum(weights_raw, axis=-1, keepdims=True))
    probability_reduced = lax.optimization_barrier(probs.astype(jnp.bfloat16)).astype(jnp.float32)
    output_results = jnp.einsum('npy,nys->nps', probability_reduced, listed_values)
    delta = lax.optimization_barrier(jnp.sum(gradient_single * output_results, axis=-1))
    probability_gradient = jnp.einsum('vwi,vri->vwr', gradient_single, listed_values)
    grad_scores = probs * (probability_gradient - delta[..., None])
    gradient_reduced = lax.optimization_barrier(grad_scores.astype(jnp.bfloat16)).astype(jnp.float32)
    query_sparse_rows = scale_factor * jnp.einsum('npy,nys->nps', gradient_reduced, listed_keys)
    key_contributions = (scale_factor * jnp.einsum('otx,otu->oxu', gradient_reduced, query_single)).reshape(SEQUENCE_BLOCKS, listed_total_count, BLOCK_TOKENS, HEAD_FEATURES)
    value_contributions = jnp.einsum('otx,otu->oxu', probability_reduced, gradient_single).reshape(SEQUENCE_BLOCKS, listed_total_count, BLOCK_TOKENS, HEAD_FEATURES)
    front = 3 + GLOBALS
    key_round = lax.optimization_barrier(key_contributions[:, front:].astype(jnp.bfloat16)).astype(jnp.float32)
    value_round = lax.optimization_barrier(value_contributions[:, front:].astype(jnp.bfloat16)).astype(jnp.float32)
    key_contributions = jnp.concatenate([key_contributions[:, :front], key_round], axis=1)
    value_contributions = jnp.concatenate([value_contributions[:, :front], value_round], axis=1)
    flat_listed = listed.reshape(-1)
    key_accum = jnp.zeros((SEQUENCE_BLOCKS + 2, BLOCK_TOKENS, HEAD_FEATURES), jnp.float32).at[flat_listed].add(key_contributions.reshape(-1, BLOCK_TOKENS, HEAD_FEATURES))
    value_accum = jnp.zeros((SEQUENCE_BLOCKS + 2, BLOCK_TOKENS, HEAD_FEATURES), jnp.float32).at[flat_listed].add(value_contributions.reshape(-1, BLOCK_TOKENS, HEAD_FEATURES))
    glob_query = query_blocks[glob_blocks].reshape(GLOBALS * BLOCK_TOKENS, HEAD_FEATURES)
    glob_grad = grad_blocks[glob_blocks].reshape(GLOBALS * BLOCK_TOKENS, HEAD_FEATURES)
    glob_scores = jnp.dot(glob_query, key_rows.T, preferred_element_type=jnp.float32) * scale_factor
    glob_exp = jnp.exp(glob_scores)
    glob_total = lax.optimization_barrier(jnp.sum(glob_exp, axis=-1))
    glob_exp_half = glob_exp.astype(jnp.bfloat16)
    glob_out = jnp.dot(glob_exp_half, value_rows, preferred_element_type=jnp.float32) / glob_total[:, None]
    glob_delta = lax.optimization_barrier(jnp.sum(glob_grad.astype(jnp.float32) * glob_out, axis=-1))
    glob_prob = glob_exp / glob_total[:, None]
    glob_prob_half = glob_prob.astype(jnp.bfloat16)
    glob_dprob = jnp.dot(glob_grad, value_rows.T, preferred_element_type=jnp.float32)
    glob_dscore = (glob_prob * (glob_dprob - glob_delta[:, None])).astype(jnp.bfloat16)
    glob_dquery = scale_factor * jnp.dot(glob_dscore, key_rows, preferred_element_type=jnp.float32)
    glob_dkey = scale_factor * jnp.dot(glob_dscore.T, glob_query, preferred_element_type=jnp.float32)
    glob_dvalue = jnp.dot(glob_prob_half.T, glob_grad, preferred_element_type=jnp.float32)
    query_full = query_sparse_rows.at[glob_blocks].set(glob_dquery.reshape(GLOBALS, BLOCK_TOKENS, HEAD_FEATURES))
    query_out = query_full.reshape(TOKENS, HEAD_FEATURES).astype(jnp.bfloat16)
    key_out = (key_accum[1:-1].reshape(TOKENS, HEAD_FEATURES) + glob_dkey).astype(jnp.bfloat16)
    value_out = (value_accum[1:-1].reshape(TOKENS, HEAD_FEATURES) + glob_dvalue).astype(jnp.bfloat16)
    return (query_out, key_out, value_out)

def reference(queries, keys, values, out_grad, out_weight, rand_blocks, glob_blocks):
    attn_grad = jnp.dot(out_grad, out_weight.T, preferred_element_type=jnp.float32).astype(jnp.bfloat16)
    is_global = jnp.zeros((SEQUENCE_BLOCKS,), dtype=bool).at[glob_blocks].set(True)

    def one_head(head_number):
        start = (head_number * HEAD_FEATURES).astype(jnp.int32)
        query_rows = lax.dynamic_slice_in_dim(queries, start, HEAD_FEATURES, 1)
        key_rows = lax.dynamic_slice_in_dim(keys, start, HEAD_FEATURES, 1)
        value_rows = lax.dynamic_slice_in_dim(values, start, HEAD_FEATURES, 1)
        grad_rows = lax.dynamic_slice_in_dim(attn_grad, start, HEAD_FEATURES, 1)
        random_row = lax.dynamic_index_in_dim(rand_blocks, head_number, 0, keepdims=False)
        return attend_head(query_rows, key_rows, value_rows, grad_rows, random_row, glob_blocks, is_global)
    query_heads, key_heads, value_heads = lax.map(one_head, jnp.arange(HEADS, dtype=jnp.int32))

    def merge_heads(stacked):
        return stacked.transpose(1, 0, 2).reshape(TOKENS, D)
    return (merge_heads(query_heads), merge_heads(key_heads), merge_heads(value_heads))
```

```python
import functools
import math

import jax
import jax.numpy as jnp
from jax import lax
from jax.experimental import pallas as pl
from jax.experimental.pallas import tpu as pltpu
from jax.sharding import PartitionSpec as P

F = 128
BT = 64
RANDOMS = 3
GLOBALS = 2
GR = GLOBALS * BT
CHUNK = 32
TINY_ROWS = 32
FLOOR = 1e-30
SCALE = 1.0 / math.sqrt(F)
BF = jnp.bfloat16
F32 = jnp.float32


VMEM = pltpu.VMEM
ANY = pl.ANY


def nt(a, b):
    return lax.dot_general(a, b, (((1,), (1,)), ((), ())), preferred_element_type=F32)


def tn(a, b):
    return lax.dot_general(a, b, (((0,), (0,)), ((), ())), preferred_element_type=F32)


def nn(a, b):
    return lax.dot_general(a, b, (((1,), (0,)), ((), ())), preferred_element_type=F32)


def params(mib=48):
    return pltpu.CompilerParams(vmem_limit_bytes=mib * 1024 * 1024)


def whole(shape):
    return pl.BlockSpec(shape, lambda *_: (0,) * len(shape))


def cost(flops, nbytes):
    return pl.CostEstimate(flops=int(flops), bytes_accessed=int(nbytes), transcendentals=0)


def pick_kernel(loc, q, k, v, o, out, sem):
    copies = []
    for a, ref in enumerate((q, k, v, o)):
        for g in range(GLOBALS):
            row = pl.multiple_of(loc[g] * BT, BT)
            copies.append(
                pltpu.make_async_copy(
                    ref.at[pl.ds(row, BT)],
                    out.at[pl.ds((a * GLOBALS + g) * BT, BT)],
                    sem.at[a * GLOBALS + g],
                )
            )
    for c in copies:
        c.start()
    for c in copies:
        c.wait()


def pack_kernel(cap, blocks, src, k, v, out):
    d = pl.program_id(0)
    for c in range(cap):
        s = jnp.maximum(src[d * cap + c], 0)
        row = pl.multiple_of((s % blocks) * BT, BT)
        col = pl.multiple_of((s // blocks) * F, F)
        out[c * 2 * BT : c * 2 * BT + BT] = k[pl.ds(row, BT), pl.ds(col, F)]
        out[c * 2 * BT + BT : (c + 1) * 2 * BT] = v[pl.ds(row, BT), pl.ds(col, F)]


def rider_kernel(n, stride, at, heads, row_ref, r, big, out, raw, buf, sem, sems):
    del big
    row = pl.multiple_of(row_ref[0], CHUNK)
    c = pltpu.make_async_copy(r.at[pl.ds(row, CHUNK)], raw, sem)
    c.start()
    c.wait()
    for h in range(heads):
        buf[h * CHUNK : (h + 1) * CHUNK] = raw[:, h * F : (h + 1) * F]
    copies = [
        pltpu.make_async_copy(
            buf, out.at[pl.ds(d * stride + at, heads * CHUNK)], sems.at[d]
        )
        for d in range(n)
    ]
    for c in copies:
        c.start()
    for c in copies:
        c.wait()


def grad_kernel(n, width, hr, w, *refs):
    out = refs[n]
    acc = None
    for j in range(n):
        col = pl.multiple_of(lax.rem(hr[0] - j + n, n) * width, width)
        part = nt(refs[j][...], w[:, pl.ds(col, width)])
        acc = part if acc is None else acc + part
    out[...] = acc.astype(BF)


def attn_kernel(
    blocks, cap, ret_rows, off, meta, q, k, v, g, lo, hi, rid, inc,
    dq, dk, dv, lot, hit, ret, kx, vx, kl, vl, kacc, vacc, kga, vga,
):
    h = pl.program_id(0)
    tokens = blocks * BT
    requests = blocks * RANDOMS * pl.num_programs(0)
    heads = 4
    win = 3 * BT
    front = win + GR
    kx[0:BT] = lo[0:BT]
    vx[0:BT] = lo[BT : 2 * BT]
    kx[BT : BT + tokens] = k[...]
    vx[BT : BT + tokens] = v[...]
    kx[BT + tokens : 2 * BT + tokens] = hi[0:BT]
    vx[BT + tokens : 2 * BT + tokens] = hi[BT : 2 * BT]
    pieces = GR // CHUNK
    for par in range(2):
        for t in range(pieces):
            at = win + t * CHUNK
            kl[par, at : at + CHUNK] = rid[
                pl.ds(pl.multiple_of((pieces + t) * heads * CHUNK + h * CHUNK, CHUNK), CHUNK)
            ]
            vl[par, at : at + CHUNK] = rid[
                pl.ds(pl.multiple_of((2 * pieces + t) * heads * CHUNK + h * CHUNK, CHUNK), CHUNK)
            ]
    kacc[...] = jnp.zeros_like(kacc)
    vacc[...] = jnp.zeros_like(vacc)
    kga[...] = jnp.zeros_like(kga)
    vga[...] = jnp.zeros_like(vga)
    for b in range(blocks):
        par = b % 2
        kl[par, 0:win] = kx[b * BT : b * BT + win]
        vl[par, 0:win] = vx[b * BT : b * BT + win]
        for r in range(RANDOMS):
            o = off[h * (blocks * RANDOMS) + b * RANDOMS + r]
            at = front + r * BT
            kl[par, at : at + BT] = inc[pl.ds(pl.multiple_of(o, 2 * BT), BT)]
            vl[par, at : at + BT] = inc[pl.ds(pl.multiple_of(o + BT, BT), BT)]
        kb = kl[par]
        vb = vl[par]
        qb = q[b * BT : (b + 1) * BT]
        gb = g[b * BT : (b + 1) * BT]
        gb = jnp.where(meta[b] != 0, jnp.zeros_like(gb), gb)
        e = jnp.exp(nt(qb, kb) * SCALE)
        if b == 0 or b == blocks - 1:
            lane = lax.broadcasted_iota(jnp.int32, e.shape, 1)
            if b == 0:
                e = jnp.where((lane < BT) & (meta[blocks] != 0), 0.0, e)
            if b == blocks - 1:
                last = (lane >= 2 * BT) & (lane < win)
                e = jnp.where(last & (meta[blocks + 1] != 0), 0.0, e)
        p = e / jnp.sum(e, axis=-1, keepdims=True)
        p16 = p.astype(BF)
        gv = nt(gb, vb)
        delta = jnp.sum(p16.astype(F32) * gv, axis=-1, keepdims=True)
        ds = (p * (gv - delta)).astype(BF)
        dq[b * BT : (b + 1) * BT] = (nn(ds, kb) * SCALE).astype(BF)
        dkl = tn(ds, qb) * SCALE
        dvl = tn(p16, gb)
        kacc[b * BT : b * BT + win] += dkl[0:win]
        vacc[b * BT : b * BT + win] += dvl[0:win]
        kga[...] += dkl[win:front]
        vga[...] += dvl[win:front]
        for r in range(RANDOMS):
            o = off[requests + h * (blocks * RANDOMS) + b * RANDOMS + r]
            at = front + r * BT
            ret[pl.ds(pl.multiple_of(o, CHUNK), BT)] = dkl[at : at + BT].astype(BF)
            ret[pl.ds(pl.multiple_of(o + BT, CHUNK), BT)] = dvl[at : at + BT].astype(BF)
    dk[...] = kacc[BT : BT + tokens]
    dv[...] = vacc[BT : BT + tokens]
    lot[0:BT] = kacc[0:BT].astype(BF)
    lot[BT : 2 * BT] = vacc[0:BT].astype(BF)
    hit[0:BT] = kacc[BT + tokens : 2 * BT + tokens].astype(BF)
    hit[BT : 2 * BT] = vacc[BT + tokens : 2 * BT + tokens].astype(BF)
    for t in range(pieces):
        base = (pieces * h + t) * ret_rows + cap * 2 * BT
        ret[pl.ds(pl.multiple_of(base, CHUNK), CHUNK)] = kga[
            t * CHUNK : (t + 1) * CHUNK
        ].astype(BF)
        ret[pl.ds(pl.multiple_of(base + CHUNK, CHUNK), CHUNK)] = vga[
            t * CHUNK : (t + 1) * CHUNK
        ].astype(BF)


def split3(x):
    a = x.astype(BF).astype(F32)
    b = (x - a).astype(BF).astype(F32)
    return a, b, x - a - b


def rows_kernel(n, hn, ret_rows, at, hr, k, v, w, qg, *refs):
    xs = refs[:hn]
    ret_in, gg_out, ret = refs[hn : hn + 3]
    ogg, ab, tf, tiny, sems, sems2 = refs[hn + 3 :]
    del ret_in
    h = pl.program_id(0)
    heads = pl.num_programs(0)
    pieces = GR // CHUNK
    cols = 4

    @pl.when(h == 0)
    def _():
        tf[...] = jnp.zeros_like(tf)
        for j in range(hn):
            col = lax.rem(hr[0] - j + hn, hn) * (cols * F)
            for t in range(pieces):
                for c in range(cols):
                    r0 = (t * cols + c) * CHUNK
                    ogg[
                        t * CHUNK : (t + 1) * CHUNK, pl.ds(pl.multiple_of(col + c * F, F), F)
                    ] = xs[j][r0 : r0 + CHUNK]

    gg = nt(ogg[...], w[...]).astype(BF)
    gg_out[...] = gg
    parts = [
        qg[pl.ds(pl.multiple_of(t * cols * CHUNK + h * CHUNK, CHUNK), CHUNK)]
        for t in range(pieces)
    ]
    qrows = jnp.concatenate(parts, axis=0)
    e = jnp.exp(nt(k[...], qrows) * SCALE)
    tot = jnp.sum(e, axis=0, keepdims=True)
    floor = jnp.maximum(tot, FLOOR)
    gv = nt(v[...], gg)
    num = jnp.sum(e.astype(BF).astype(F32) * gv, axis=0, keepdims=True)
    delta = num / floor
    p = e / floor
    ab[0] = (tn((p * (gv - delta)).astype(BF), k[...]) * SCALE).astype(BF)
    ab[1] = (tn(p.astype(BF), k[...]) * SCALE).astype(BF)
    for i, piece in enumerate(split3(tot)):
        tf[pl.ds(3 * h + i, 1)] = piece
    for i, piece in enumerate(split3(delta)):
        tf[pl.ds(12 + 3 * h + i, 1)] = piece
    copies = []
    for a in range(2):
        for t in range(pieces):
            row = (pieces * h + t) * ret_rows + at + (2 + a) * CHUNK
            copies.append(
                pltpu.make_async_copy(
                    ab.at[a, pl.ds(t * CHUNK, CHUNK)],
                    ret.at[pl.ds(pl.multiple_of(row, CHUNK), CHUNK)],
                    sems.at[a * pieces + t],
                )
            )
    for c in copies:
        c.start()
    for c in copies:
        c.wait()

    @pl.when(h == heads - 1)
    def _():
        tiny[...] = tf[...].astype(BF)
        more = [
            pltpu.make_async_copy(
                tiny, ret.at[pl.ds(d * ret_rows + at + 4 * CHUNK, TINY_ROWS)], sems2.at[d]
            )
            for d in range(n)
        ]
        for c in more:
            c.start()
        for c in more:
            c.wait()


def sum_kernel(n, at, rows, heads, rank, back, out, stats, buf, tf, wide, sem):
    c = pltpu.make_async_copy(back.at[:, pl.ds(at, rows), :], buf, sem)
    c.start()
    c.wait()
    pieces = GR // CHUNK
    t = rank[0] % pieces
    hh = rank[0] // pieces
    tf[...] = buf[:, 4 * CHUNK : 4 * CHUNK + TINY_ROWS].astype(F32)
    wide[...] = jnp.zeros_like(wide)
    stats[...] = jnp.zeros_like(stats)
    for h in range(heads):
        tot = [tf[s, 3 * h : 3 * h + 1] + tf[s, 3 * h + 1 : 3 * h + 2] + tf[s, 3 * h + 2 : 3 * h + 3] for s in range(n)]
        dl = [tf[s, 12 + 3 * h : 13 + 3 * h] + tf[s, 13 + 3 * h : 14 + 3 * h] + tf[s, 14 + 3 * h : 15 + 3 * h] for s in range(n)]
        tot = jnp.concatenate(tot, axis=0)
        dl = jnp.concatenate(dl, axis=0)
        total = jnp.sum(tot, axis=0, keepdims=True)
        share = jnp.maximum(tot, FLOOR) / total
        delta = jnp.sum(share * dl, axis=0, keepdims=True)
        stats[h : h + 1] = total
        stats[heads + h : heads + h + 1] = delta
        wide[h, 0:n] = share
        wide[h, n : 2 * n] = share * (dl - delta)
    flipped = jnp.transpose(wide[hh])
    wide[0] = flipped
    cf = wide[0, pl.ds(pl.multiple_of(t * CHUNK, CHUNK), CHUNK)]
    dq = jnp.zeros((CHUNK, F), F32)
    kt = jnp.zeros((CHUNK, F), F32)
    vt = jnp.zeros((CHUNK, F), F32)
    for s in range(n):
        kt = kt + buf[s, 0:CHUNK].astype(F32)
        vt = vt + buf[s, CHUNK : 2 * CHUNK].astype(F32)
        dq = dq + cf[:, s : s + 1] * buf[s, 2 * CHUNK : 3 * CHUNK].astype(F32)
        dq = dq + cf[:, n + s : n + s + 1] * buf[s, 3 * CHUNK : 4 * CHUNK].astype(F32)
    z = [x.astype(BF) for x in (dq, kt, vt)]
    for d in range(n):
        for i in range(3):
            out[(d * 3 + i) * CHUNK : (d * 3 + i + 1) * CHUNK] = z[i]


def final_kernel(
    cap, blocks, heads, src, loc, back, dk, dv, lo, hi, k, v, qg, gg, stats,
    kout, vout, fix, kacc, vacc,
):
    s = pl.program_id(0)
    pieces = GR // CHUNK
    tokens = blocks * BT

    @pl.when(s == 0)
    def _():
        kacc[...] = dk[...]
        vacc[...] = dv[...]

    for c in range(cap):
        sr = src[s * cap + c]

        @pl.when(sr >= 0)
        def _(sr=sr, c=c):
            rows = pl.ds(pl.multiple_of(sr * BT, BT), BT)
            kacc[rows] += back[c * 2 * BT : c * 2 * BT + BT].astype(F32)
            vacc[rows] += back[c * 2 * BT + BT : (c + 1) * 2 * BT].astype(F32)

    @pl.when(s == pl.num_programs(0) - 1)
    def _():
        for h in range(heads):
            cs = slice(h * F, (h + 1) * F)
            first = h * tokens
            last = first + tokens - BT
            kacc[first : first + BT] += lo[0:BT, cs].astype(F32)
            vacc[first : first + BT] += lo[BT : 2 * BT, cs].astype(F32)
            kacc[last : last + BT] += hi[0:BT, cs].astype(F32)
            vacc[last : last + BT] += hi[BT : 2 * BT, cs].astype(F32)
            qrows = jnp.concatenate(
                [qg[(t * heads + h) * CHUNK : (t * heads + h + 1) * CHUNK] for t in range(pieces)],
                axis=0,
            )
            grows = gg[:, cs]
            total = stats[h : h + 1]
            delta = stats[heads + h : heads + h + 1]
            pg = jnp.exp(nt(k[:, cs], qrows) * SCALE) / total
            dsg = (pg * (nt(v[:, cs], grows) - delta)).astype(BF)
            kt = kacc[first : first + tokens] + nn(dsg, qrows) * SCALE
            vt = vacc[first : first + tokens] + nn(pg.astype(BF), grows)
            kout[:, cs] = kt.astype(BF)
            vout[:, cs] = vt.astype(BF)
            kacc[first : first + tokens] = kt
            vacc[first : first + tokens] = vt
            for g in range(GLOBALS):
                rows = pl.ds(pl.multiple_of(first + loc[g] * BT, BT), BT)
                fix[g * 2 * BT : g * 2 * BT + BT, cs] = kacc[rows]
                fix[g * 2 * BT + BT : (g + 1) * 2 * BT, cs] = vacc[rows]


def fix_kernel(heads, meta, gath, fix, qi, ki, vi, qo, ko, vo, buf, sems):
    del qi, ki, vi
    half = BT // CHUNK
    pieces = GR // CHUNK
    for g in range(GLOBALS):

        @pl.when(meta[g] != 0)
        def _(g=g):
            for h in range(heads):
                cs = slice(h * F, (h + 1) * F)
                for u in range(half):
                    base = (h * pieces + g * half + u) * 3 * CHUNK
                    r = slice(u * CHUNK, (u + 1) * CHUNK)
                    f0 = g * 2 * BT + u * CHUNK
                    buf[0, r, cs] = gath[base : base + CHUNK]
                    buf[1, r, cs] = (
                        fix[f0 : f0 + CHUNK, cs] + gath[base + CHUNK : base + 2 * CHUNK].astype(F32)
                    ).astype(BF)
                    buf[2, r, cs] = (
                        fix[f0 + BT : f0 + BT + CHUNK, cs]
                        + gath[base + 2 * CHUNK : base + 3 * CHUNK].astype(F32)
                    ).astype(BF)
            rows = pl.ds(pl.multiple_of(meta[GLOBALS + g] * BT, BT), BT)
            copies = [
                pltpu.make_async_copy(buf.at[i], o.at[rows], sems.at[i])
                for i, o in enumerate((qo, ko, vo))
            ]
            for c in copies:
                c.start()
            for c in copies:
                c.wait()


def body(queries, keys, values, out_grad, out_weight, rand_blocks, glob_blocks):
    tokens, width = queries.shape
    heads = width // F
    blocks = tokens // BT
    n = lax.axis_size("seq")
    hn = lax.axis_size("head")
    rank = lax.axis_index("seq").astype(jnp.int32)
    hr = lax.axis_index("head").astype(jnp.int32)
    per_head = blocks * RANDOMS
    requests = per_head * heads
    cap = 3 * requests // (2 * n)
    slot_rows = cap * 2 * BT
    rider = heads * CHUNK
    big_rows = slot_rows + rider
    ret_rows = slot_rows + 4 * CHUNK + TINY_ROWS
    pieces = GR // CHUNK
    sds = jax.ShapeDtypeStruct

    def to_heads(x):
        return [x] + [
            lax.ppermute(x, "head", [(i, (i + j) % hn) for i in range(hn)]) for j in range(1, hn)
        ]

    def up(x):
        return lax.ppermute(x, "seq", [(i, i + 1) for i in range(n - 1)])

    def down(x):
        return lax.ppermute(x, "seq", [(i + 1, i) for i in range(n - 1)])

    def exchange(x):
        return lax.all_to_all(x, "seq", split_axis=0, concat_axis=0, tiled=True)

    grads = to_heads(out_grad)
    edge_lo = up(jnp.concatenate([keys[-BT:], values[-BT:]], axis=0))
    edge_hi = down(jnp.concatenate([keys[:BT], values[:BT]], axis=0))

    owner = glob_blocks // blocks
    loc = glob_blocks % blocks
    owned = owner == rank
    picked = pl.pallas_call(
        pick_kernel,
        out_shape=sds((4 * GR, width), BF),
        grid_spec=pltpu.PrefetchScalarGridSpec(
            num_scalar_prefetch=1,
            in_specs=[pl.BlockSpec(memory_space=ANY)] * 4,
            out_specs=pl.BlockSpec(memory_space=VMEM),
            scratch_shapes=[pltpu.SemaphoreType.DMA((4 * GLOBALS,))],
        ),
        compiler_params=params(),
        name="pick",
    )(loc, queries, keys, values, out_grad)
    scattered = exchange(picked)

    every = (
        rand_blocks.reshape(heads, n, per_head).transpose(1, 0, 2).reshape(n, requests)
    )
    order = jnp.arange(requests, dtype=jnp.int32)
    before = (order[:, None] < order[None, :]).astype(BF)
    asked = every // blocks == rank
    asked_rank = jnp.dot(asked.astype(BF), before, preferred_element_type=F32).astype(jnp.int32)
    slots = jnp.arange(cap, dtype=jnp.int32)
    matched = asked[:, None, :] & (asked_rank[:, None, :] == slots[None, :, None])
    value = order[None, :] // per_head * blocks + every % blocks + 1
    src = (jnp.sum(jnp.where(matched, value[:, None, :], 0), axis=-1) - 1).reshape(n * cap)
    mine = lax.dynamic_index_in_dim(every, rank, 0, keepdims=False)
    want = mine // blocks
    same = (want[:, None] == want[None, :]) & (order[:, None] > order[None, :])
    slot = jnp.sum(same.astype(jnp.int32), axis=1)
    off = jnp.concatenate(
        [want * big_rows + slot * (2 * BT), want * ret_rows + slot * (2 * BT)]
    )

    big = pl.pallas_call(
        functools.partial(pack_kernel, cap, blocks),
        out_shape=sds((n * big_rows, F), BF),
        grid_spec=pltpu.PrefetchScalarGridSpec(
            num_scalar_prefetch=1,
            grid=(n,),
            in_specs=[whole((tokens, width)), whole((tokens, width))],
            out_specs=pl.BlockSpec((big_rows, F), lambda d, *_: (d, 0)),
        ),
        compiler_params=params(),
        cost_estimate=cost(0, 2 * n * big_rows * F * 2),
        name="pack",
    )(src, keys, values)
    piece_owner = jnp.where((rank % pieces) // (pieces // GLOBALS) == 0, owner[0], owner[1])
    big = pl.pallas_call(
        functools.partial(rider_kernel, n, big_rows, slot_rows, heads),
        out_shape=sds((n * big_rows, F), BF),
        grid_spec=pltpu.PrefetchScalarGridSpec(
            num_scalar_prefetch=1,
            in_specs=[pl.BlockSpec(memory_space=ANY)] * 2,
            out_specs=pl.BlockSpec(memory_space=ANY),
            scratch_shapes=[
                VMEM((CHUNK, width), BF),
                VMEM((rider, F), BF),
                pltpu.SemaphoreType.DMA,
                pltpu.SemaphoreType.DMA((n,)),
            ],
        ),
        input_output_aliases={2: 0},
        compiler_params=params(),
        name="rider",
    )((piece_owner * CHUNK).reshape(1), scattered, big)
    inc = exchange(big)
    rid = inc.reshape(n, big_rows, F)[:, slot_rows:].reshape(n * rider, F)

    rows_per = pieces * rider
    row_grads = to_heads(rid[3 * rows_per : 4 * rows_per])
    q_rows = rid[:rows_per]

    tile = tokens // 4
    attn_grad = pl.pallas_call(
        functools.partial(grad_kernel, hn, width),
        out_shape=sds((tokens, width), BF),
        grid_spec=pltpu.PrefetchScalarGridSpec(
            num_scalar_prefetch=1,
            grid=(4,),
            in_specs=[whole(out_weight.shape)]
            + [pl.BlockSpec((tile, width), lambda i, *_: (i, 0))] * hn,
            out_specs=pl.BlockSpec((tile, width), lambda i, *_: (i, 0)),
        ),
        compiler_params=params(),
        cost_estimate=cost(2 * tokens * width * width * hn, 9 * 2**20),
        name="grad",
    )(hr.reshape(1), out_weight, *grads)

    is_global = (
        rank * blocks + jnp.arange(blocks, dtype=jnp.int32)[:, None] == glob_blocks[None, :]
    ).any(axis=1)
    meta = jnp.concatenate(
        [
            is_global.astype(jnp.int32),
            (rank == 0).astype(jnp.int32).reshape(1),
            (rank == n - 1).astype(jnp.int32).reshape(1),
        ]
    )
    head_block = pl.BlockSpec((tokens, F), lambda h, *_: (0, h))
    edge_block = pl.BlockSpec((2 * BT, F), lambda h, *_: (0, h))
    sum_block = pl.BlockSpec((tokens, F), lambda h, *_: (h, 0))
    dq, dk, dv, lo_terms, hi_terms, ret = pl.pallas_call(
        functools.partial(attn_kernel, blocks, cap, ret_rows),
        out_shape=(
            sds((tokens, width), BF),
            sds((heads * tokens, F), F32),
            sds((heads * tokens, F), F32),
            sds((2 * BT, width), BF),
            sds((2 * BT, width), BF),
            sds((n * ret_rows, F), BF),
        ),
        grid_spec=pltpu.PrefetchScalarGridSpec(
            num_scalar_prefetch=2,
            grid=(heads,),
            in_specs=[
                head_block, head_block, head_block, head_block, edge_block, edge_block,
                whole(rid.shape), whole(inc.shape),
            ],
            out_specs=(
                head_block, sum_block, sum_block, edge_block, edge_block,
                whole((n * ret_rows, F)),
            ),
            scratch_shapes=[
                VMEM((tokens + 2 * BT, F), BF),
                VMEM((tokens + 2 * BT, F), BF),
                VMEM((2, 3 * BT + GR + RANDOMS * BT, F), BF),
                VMEM((2, 3 * BT + GR + RANDOMS * BT, F), BF),
                VMEM((tokens + 2 * BT, F), F32),
                VMEM((tokens + 2 * BT, F), F32),
                VMEM((GR, F), F32),
                VMEM((GR, F), F32),
            ],
        ),
        compiler_params=params(),
        cost_estimate=cost(10 * requests // 3 * BT * 512 * F, 16 * 2**20),
        name="attn",
    )(off, meta, queries, keys, values, attn_grad, edge_lo, edge_hi, rid, inc)
    from_above = down(lo_terms)
    from_below = up(hi_terms)

    gg, ret = pl.pallas_call(
        functools.partial(rows_kernel, n, hn, ret_rows, slot_rows),
        out_shape=(sds((GR, width), BF), sds((n * ret_rows, F), BF)),
        grid_spec=pltpu.PrefetchScalarGridSpec(
            num_scalar_prefetch=1,
            grid=(heads,),
            in_specs=[
                head_block,
                head_block,
                pl.BlockSpec((F, out_weight.shape[1]), lambda h, *_: (h, 0)),
                whole(q_rows.shape),
            ]
            + [whole(q_rows.shape)] * hn
            + [pl.BlockSpec(memory_space=ANY)],
            out_specs=(
                pl.BlockSpec((GR, F), lambda h, *_: (0, h)),
                pl.BlockSpec(memory_space=ANY),
            ),
            scratch_shapes=[
                VMEM((GR, out_weight.shape[1]), BF),
                VMEM((2, GR, F), BF),
                VMEM((TINY_ROWS, F), F32),
                VMEM((TINY_ROWS, F), BF),
                pltpu.SemaphoreType.DMA((2 * pieces,)),
                pltpu.SemaphoreType.DMA((n,)),
            ],
        ),
        input_output_aliases={5 + hn: 1},
        compiler_params=params(),
        cost_estimate=cost(2 * 10**9, 8 * 2**20),
        name="rows",
    )(hr.reshape(1), keys, values, out_weight, q_rows, *row_grads, ret)
    back = exchange(ret)

    tail = 4 * CHUNK + TINY_ROWS
    mixed, stats = pl.pallas_call(
        functools.partial(sum_kernel, n, slot_rows, tail, heads),
        out_shape=(sds((n * 3 * CHUNK, F), BF), sds((2 * heads, F), F32)),
        grid_spec=pltpu.PrefetchScalarGridSpec(
            num_scalar_prefetch=1,
            in_specs=[pl.BlockSpec(memory_space=ANY)],
            out_specs=(pl.BlockSpec(memory_space=VMEM), pl.BlockSpec(memory_space=VMEM)),
            scratch_shapes=[
                VMEM((n, tail, F), BF),
                VMEM((n, TINY_ROWS, F), F32),
                VMEM((heads, F, F), F32),
                pltpu.SemaphoreType.DMA,
            ],
        ),
        compiler_params=params(),
        name="mix",
    )(rank.reshape(1), back.reshape(n, ret_rows, F))
    gathered = exchange(mixed)

    key_grad, value_grad, fix = pl.pallas_call(
        functools.partial(final_kernel, cap, blocks, heads),
        out_shape=(
            sds((tokens, width), BF),
            sds((tokens, width), BF),
            sds((2 * GR, width), F32),
        ),
        grid_spec=pltpu.PrefetchScalarGridSpec(
            num_scalar_prefetch=2,
            grid=(n,),
            in_specs=[
                pl.BlockSpec((ret_rows, F), lambda s, *_: (s, 0)),
                whole((heads * tokens, F)),
                whole((heads * tokens, F)),
                whole((2 * BT, width)),
                whole((2 * BT, width)),
                whole((tokens, width)),
                whole((tokens, width)),
                whole(q_rows.shape),
                whole((GR, width)),
                whole((2 * heads, F)),
            ],
            out_specs=(
                whole((tokens, width)), whole((tokens, width)), whole((2 * GR, width)),
            ),
            scratch_shapes=[VMEM((heads * tokens, F), F32), VMEM((heads * tokens, F), F32)],
        ),
        compiler_params=params(),
        cost_estimate=cost(10**9, 14 * 2**20),
        name="final",
    )(src, loc, back, dk, dv, from_below, from_above, keys, values, q_rows, gg, stats)

    whom = jnp.concatenate([owned.astype(jnp.int32), loc])
    return pl.pallas_call(
        functools.partial(fix_kernel, heads),
        out_shape=tuple(sds((tokens, width), BF) for _ in range(3)),
        grid_spec=pltpu.PrefetchScalarGridSpec(
            num_scalar_prefetch=1,
            in_specs=[pl.BlockSpec(memory_space=VMEM)] * 2 + [pl.BlockSpec(memory_space=ANY)] * 3,
            out_specs=tuple(pl.BlockSpec(memory_space=ANY) for _ in range(3)),
            scratch_shapes=[VMEM((3, BT, width), BF), pltpu.SemaphoreType.DMA((3,))],
        ),
        input_output_aliases={3: 0, 4: 1, 5: 2},
        compiler_params=params(),
        name="fix",
    )(whom, gathered, fix, dq, key_grad, value_grad)


def solution(mesh):
    in_specs = (
        P("seq", "head"),
        P("seq", "head"),
        P("seq", "head"),
        P("seq", "head"),
        P("head", None),
        P("head", None, None),
        P(),
    )
    out_specs = (P("seq", "head"), P("seq", "head"), P("seq", "head"))
    return jax.shard_map(body, mesh=mesh, in_specs=in_specs, out_specs=out_specs, check_vma=False)
```
